256 devices in a mesh: tile: 64 (over z, x, y_lo), lev: 4 (over y_hi, core).
Axes of the slice: x: 4, y: 4 (y_hi: 2, y_lo: 2; y = y_hi * 2 + y_lo), z: 8, core: 2. Of those that a mesh axis runs over, the one named last changes fastest.
Arguments:
- cotangent: float32 [64, 88, 128, 128], P('tile', 'lev'), may hold values from -6 to 6
- surface_cotangent: float32 [64, 128, 128], P('tile'), may hold values from -6 to 6
- helmholtz_diagonal: float32 [64, 128, 128], P('tile'), may hold values from 0.05 to 0.5
- coefficients: bfloat16 [64, 4, 88, 128, 128], P('tile', None, 'lev'), may hold values from 0.029907227 to 0.5
- vertical_inverse: float32 [64, 88, 88], P('tile'), may hold values from -0.625 to 0.625
- layer_thickness: float32 [88], replicated, may hold values from 0.2 to 2
- edge_flips: int32 [64, 4], replicated, may hold values from 0 to 1, as said below
- land_tiles: int32 [64], replicated, may hold values 0 or 1
Outputs:
- theta_adjoint: float32 [64, 88, 128, 128], P('tile', 'lev')
- surface_adjoint: float32 [64, 128, 128], P('tile')
The draws below stay inside these ranges and needn't reach their ends.
Inputs may be any that keep to these rules, and one draw needn't show every extreme that they name: Columns 0 to 3 flag the east, west, north and south edge; 1 means the neighbour's edge runs in the opposite order. edge_flips[t,1] equals edge_flips[(t-1) mod 64,0] and edge_flips[t,3] equals edge_flips[(t-4) mod 64,2]. `land_tiles`: 1 marks a tile that is all land.
All inputs are finite; a program needn't handle non-finite values.
Results may differ from the reference program's by a relative error of at most 0.0003.
Values sent between devices are 32-bit elements; how exact they have to be, the bound alone decides.
A program may use at most 64 MiB of HBM per device.

```python
import math
import jax
import jax.numpy as jnp
from jax import lax

SIDE = 128
LEVELS = 88
TILE_ROW = 4
ITERS = 3
TILES = 64


def draw_edge_flips(key, part):
    eastern = jax.random.randint(jax.random.fold_in(key, 11), (TILES,), 0, 2)
    northern = jax.random.randint(jax.random.fold_in(key, 12), (TILES,), 0, 2)
    western = jnp.roll(eastern, 1)
    southern = jnp.roll(northern, TILE_ROW)
    return jnp.stack([eastern, western, northern, southern], axis=1).astype(jnp.int32)


def place_ends(values, stream_key, least, top_value):
    extent = values.shape
    index_at = [jax.random.randint(jax.random.fold_in(stream_key, axis), (), 0, extent[axis]) for axis in range(len(extent))]
    values = values.at[tuple(index_at)].set(least)
    longest = extent.index(max(extent))
    index_at[longest] = (index_at[longest] + 1) % extent[longest]
    return values.at[tuple(index_at)].set(top_value)


def block_levels(stream_key, dims, pieces, least, largest):
    level, own = 1.0, jax.random.fold_in(stream_key, 6)
    for position, blocks in pieces:
        steps = jnp.exp(jax.random.uniform(jax.random.fold_in(own, position), (blocks,), jnp.float32, least / len(pieces), largest / len(pieces)))
        level = level * jnp.repeat(steps, dims[position] // blocks).reshape([-1 if axis == position else 1 for axis in range(len(dims))])
    return level


def scatter_about(stream_key, shape, deviation, bound, split=(), held_as=jnp.bfloat16):
    factor_of = block_levels(stream_key, shape, split, -0.22, 0.18) if split else 1.0
    values = jax.random.normal(stream_key, shape, jnp.float32) * deviation * factor_of
    return jnp.minimum(jnp.maximum(values, -bound), bound).astype(held_as)


def setup_inputs(seed: int = 0) -> dict:
    arg_keys = jax.random.split(jax.random.key(seed), 9)
    return {
        "cotangent": scatter_about(arg_keys[0], (TILES, LEVELS, SIDE, SIDE), 1.0, 6.0, ((0, 64), (1, 4)), jnp.float32),
        "surface_cotangent": scatter_about(arg_keys[1], (TILES, SIDE, SIDE), 1.0, 6.0, ((0, 64),), jnp.float32),
        "helmholtz_diagonal": jnp.clip(jnp.exp(math.log(0.5) - 2.3025851 * jax.random.uniform(arg_keys[2], (TILES, SIDE, SIDE), jnp.float32) ** block_levels(arg_keys[2], (TILES, SIDE, SIDE), ((0, 64),), -0.2, 0.2)), 0.05, 0.5),
        "coefficients": jnp.clip(jnp.exp(math.log(0.5) - 2.816508 * jax.random.uniform(arg_keys[3], (TILES, 4, LEVELS, SIDE, SIDE), jnp.float32) ** block_levels(arg_keys[3], (TILES, 4, LEVELS, SIDE, SIDE), ((0, 64), (2, 4)), -0.2, 0.2)), 0.029907227, 0.5).astype(jnp.bfloat16),
        "vertical_inverse": scatter_about(arg_keys[4], (TILES, LEVELS, LEVELS), LEVELS ** -0.5, 0.625, ((0, 64),), jnp.float32),
        "layer_thickness": jnp.clip(jnp.exp(jax.random.uniform(arg_keys[5], (LEVELS,), jnp.float32, math.log(0.2), math.log(2.0))), 0.2, 2.0),
        "edge_flips": draw_edge_flips(jax.random.fold_in(arg_keys[8], 71), 0),
        "land_tiles": place_ends((jax.random.randint(arg_keys[7], (TILES,), 0, 8) < 1).astype(jnp.int32), jax.random.fold_in(arg_keys[7], 1), 0, 1),
    }


def from_neighbour(strips, offset, flags):
    moved = jnp.roll(strips, -offset, axis=0)
    shaped = flags.reshape((-1,) + (1,) * (strips.ndim - 1))
    return jnp.where(shaped == 1, jnp.flip(moved, axis=-1), moved)


def helmholtz(field, helmholtz_diagonal, edge_flips):
    east_ghost = from_neighbour(field[:, :, 0], 1, edge_flips[:, 0])
    west_ghost = from_neighbour(field[:, :, -1], -1, edge_flips[:, 1])
    north_ghost = from_neighbour(field[:, 0, :], TILE_ROW, edge_flips[:, 2])
    south_ghost = from_neighbour(field[:, -1, :], -TILE_ROW, edge_flips[:, 3])
    eastern = jnp.concatenate([field[:, :, 1:], east_ghost[:, :, None]], axis=2)
    western = jnp.concatenate([west_ghost[:, :, None], field[:, :, :-1]], axis=2)
    northern = jnp.concatenate([field[:, 1:, :], north_ghost[:, None, :]], axis=1)
    southern = jnp.concatenate([south_ghost[:, None, :], field[:, :-1, :]], axis=1)
    return (4.0 + helmholtz_diagonal) * field - (eastern + western + northern + southern)


def level_adjoint(inputs):
    adjoint, coeffs, east_ghost, west_ghost, north_ghost, south_ghost, ocean = inputs
    coeffs = coeffs.astype(jnp.float32)
    from_east = jnp.concatenate([coeffs[1][:, :, 1:] * adjoint[:, :, 1:], east_ghost[:, :, None]], axis=2)
    from_west = jnp.concatenate([west_ghost[:, :, None], coeffs[0][:, :, :-1] * adjoint[:, :, :-1]], axis=2)
    from_north = jnp.concatenate([coeffs[3][:, 1:, :] * adjoint[:, 1:, :], north_ghost[:, None, :]], axis=1)
    from_south = jnp.concatenate([south_ghost[:, None, :], coeffs[2][:, :-1, :] * adjoint[:, :-1, :]], axis=1)
    total = coeffs[0] + coeffs[1] + coeffs[2] + coeffs[3]
    return ocean * (adjoint - total * adjoint + from_east + from_west + from_north + from_south)


def vertical(inputs):
    inverse, column = inputs
    return jnp.einsum("mk,mji->kji", inverse, column, precision=lax.Precision.HIGHEST)


def reference(cotangent, surface_cotangent, helmholtz_diagonal, coefficients, vertical_inverse, layer_thickness, edge_flips, land_tiles):
    ocean_mask = (1 - land_tiles).astype(jnp.float32)
    solution = jnp.zeros_like(surface_cotangent)
    residual = surface_cotangent
    direction = surface_cotangent
    norm_now = jnp.sum(residual * residual)
    for iteration in range(ITERS):
        image = helmholtz(direction, helmholtz_diagonal, edge_flips)
        alpha = norm_now / jnp.sum(direction * image)
        solution = solution + alpha * direction
        residual = residual - alpha * image
        norm_next = jnp.sum(residual * residual)
        direction = residual + (norm_next / norm_now) * direction
        norm_now = norm_next
    shifted = cotangent + layer_thickness[None, :, None, None] * solution[:, None]
    adjoint = lax.map(vertical, (vertical_inverse, shifted))
    east_strip = coefficients[:, 1, :, :, 0].astype(jnp.float32) * adjoint[:, :, :, 0]
    west_strip = coefficients[:, 0, :, :, -1].astype(jnp.float32) * adjoint[:, :, :, -1]
    north_strip = coefficients[:, 3, :, 0, :].astype(jnp.float32) * adjoint[:, :, 0, :]
    south_strip = coefficients[:, 2, :, -1, :].astype(jnp.float32) * adjoint[:, :, -1, :]
    east_ghost = from_neighbour(east_strip, 1, edge_flips[:, 0])
    west_ghost = from_neighbour(west_strip, -1, edge_flips[:, 1])
    north_ghost = from_neighbour(north_strip, TILE_ROW, edge_flips[:, 2])
    south_ghost = from_neighbour(south_strip, -TILE_ROW, edge_flips[:, 3])
    result = lax.map(level_adjoint, (adjoint, coefficients, east_ghost, west_ghost, north_ghost, south_ghost, ocean_mask))
    return result, solution
```

```python
import functools

import jax
import jax.numpy as jnp
from jax import lax
from jax.experimental import pallas as pl
from jax.experimental.pallas import tpu as pltpu
from jax.sharding import PartitionSpec as P

MESH = pl.DeviceIdType.MESH
S = 128
NL = 22
R = 8
NC = S // R
F32 = jnp.float32
BF16 = jnp.bfloat16
HIGHEST = lax.Precision.HIGHEST


def dot(a, b, precision=None):
    return lax.dot_general(
        a, b, (((1,), (0,)), ((), ())), precision=precision, preferred_element_type=F32
    )


def dot_t(a, b, precision=None):
    return lax.dot_general(
        a, b, (((1,), (1,)), ((), ())), precision=precision, preferred_element_type=F32
    )


def iota(shape, axis):
    return lax.broadcasted_iota(jnp.int32, shape, axis)


def step_lengths(mu):
    def product(a, b, power):
        total = None
        for i, x in enumerate(a):
            for j, y in enumerate(b):
                if x is not None and y is not None:
                    term = x * y * mu[i + j + power]
                    total = term if total is None else total + term
        return total

    one = jnp.ones_like(mu[0])
    residual, direction = [one, None, None], [one, None, None]
    answer = [None, None, None]
    norm = mu[0]
    for step in range(3):
        curvature = product(direction, direction, 1)
        alpha = norm / curvature
        if step:
            alpha = jnp.where(
                jnp.logical_and(norm > 0, curvature > 0), jnp.clip(alpha, 0.1, 21.0), 0.0
            )
        for i in range(step + 1):
            term = alpha * direction[i]
            answer[i] = term if answer[i] is None else answer[i] + term
        if step < 2:
            for i in range(step, -1, -1):
                term = alpha * direction[i]
                residual[i + 1] = -term if residual[i + 1] is None else residual[i + 1] - term
            new = product(residual, residual, 0)
            beta = jnp.where(norm > 0, jnp.maximum(new, 0.0) / norm, 0.0)
            direction = [
                None if r is None else (r if d is None else r + beta * d)
                for r, d in zip(residual, direction)
            ]
            norm = new
    return answer


def kernel(
    flips,
    land,
    cot,
    surface,
    helm,
    coef_hbm,
    inverse_hbm,
    thick_hbm,
    theta,
    answer,
    gathered,
    coef,
    rhs,
    diag,
    inverse,
    thick,
    basis,
    perm,
    ring_out,
    ring_in,
    part,
    plane_slots,
    plane_total,
    z_slots,
    kron,
    weight,
    adjoint,
    strips_out,
    strips_in,
    result,
    load_sem,
    far_send,
    far_recv,
    near_send,
    near_recv,
    hand_send,
    hand_recv,
    halo_send,
    halo_recv,
    sum_send,
    sum_recv,
    ghost_send,
    ghost_recv,
    store_sem,
):
    t = lax.axis_index("tile")
    lev = lax.axis_index("lev")
    opposite = lax.rem(lev + 2, 4)
    partner = lev + 1 - 2 * lax.rem(lev, 2)
    far_partner = lax.rem(partner + 2, 4)
    z = t // 8
    q = lax.rem(t, 8)
    halo = [
        (lax.rem(t + 63, 64), lev),
        (lax.rem(t + 1, 64), lev),
        (lax.rem(t + 60, 64), lev),
        (lax.rem(t + 4, 64), lev),
    ]
    plane_peer = [(z * 8 + lax.rem(q + i, 8), lev) for i in range(1, 8)]
    z_peer = [(lax.rem(t + 8 * i, 64), lev) for i in range(1, 8)]

    barrier = pltpu.get_barrier_semaphore()
    peers = halo + plane_peer + z_peer + [(t, opposite), (t, partner)]
    for peer in peers:
        pl.semaphore_signal(barrier, inc=1, device_id=peer, device_id_type=MESH)

    def remote(src, dst, send, recv, peer):
        return pltpu.make_async_remote_copy(
            src_ref=src, dst_ref=dst, send_sem=send, recv_sem=recv,
            device_id=peer, device_id_type=MESH,
        )

    mine = pl.ds(lev * NL, NL)
    loads = [
        pltpu.make_async_copy(surface.at[0], rhs, load_sem.at[0]),
        pltpu.make_async_copy(helm.at[0], diag, load_sem.at[1]),
        pltpu.make_async_copy(inverse_hbm.at[0], inverse, load_sem.at[2]),
        pltpu.make_async_copy(thick_hbm, thick, load_sem.at[3]),
        pltpu.make_async_copy(cot.at[0], gathered.at[mine], load_sem.at[4]),
        pltpu.make_async_copy(coef_hbm.at[0], coef, load_sem.at[5]),
    ]
    for load in loads:
        load.start()

    row = iota((S, S), 0)
    lane = iota((S, S), 1)
    eye = (row == lane).astype(F32)
    anti = (row + lane == S - 1).astype(F32)
    for side in range(4):
        perm[side] = jnp.where(flips[t, side] == 1, anti, eye)

    far = []

    def send_far(chunk):
        rows = pl.ds(chunk * R, R)
        copy = remote(
            cot.at[0, :, rows, :],
            gathered.at[mine, rows, :],
            far_send.at[chunk],
            far_recv.at[chunk],
            (t, opposite),
        )
        copy.start()
        far.append(copy)

    def to_row(column):
        return jnp.sum(jnp.broadcast_to(column, (S, S)) * eye, axis=0, keepdims=True)

    halos = []

    def send_halo(turn, field):
        strips = (
            to_row(field[:, 0:1]),
            to_row(field[:, S - 1 : S]),
            field[0:1, :],
            field[S - 1 : S, :],
        )
        for side in range(4):
            slot = turn * 4 + side
            ring_out[slot] = strips[side]
        for side in range(4):
            slot = turn * 4 + side
            copy = remote(
                ring_out.at[slot], ring_in.at[slot],
                halo_send.at[slot], halo_recv.at[slot], halo[side],
            )
            copy.start()
            halos.append(copy)

    def neighbours(field):
        east = jnp.where(lane == S - 1, 0.0, pltpu.roll(field, S - 1, 1))
        west = jnp.where(lane == 0, 0.0, pltpu.roll(field, 1, 1))
        north = jnp.where(row == S - 1, 0.0, pltpu.roll(field, S - 1, 0))
        south = jnp.where(row == 0, 0.0, pltpu.roll(field, 1, 0))
        return (east + west) + (north + south)

    def to_column(line, side):
        return jnp.sum(perm[side] * line, axis=1, keepdims=True)

    def turned(line, side):
        return dot(jnp.broadcast_to(line, (8, S)), perm[side], HIGHEST)[0:1, :]

    def ghosts(lines):
        return (
            jnp.where(lane == S - 1, to_column(lines[0], 0), 0.0)
            + jnp.where(lane == 0, to_column(lines[1], 1), 0.0)
        ) + (
            jnp.where(row == S - 1, turned(lines[2], 2), 0.0)
            + jnp.where(row == 0, turned(lines[3], 3), 0.0)
        )

    def moment(a, b):
        return jnp.sum(a * b, axis=0, keepdims=True)

    loads[0].wait()
    loads[1].wait()
    pl.semaphore_wait(barrier, len(peers))

    near = remote(
        cot.at[0], gathered.at[mine], near_send.at[0], near_recv.at[0], (t, partner)
    )
    basis[0] = rhs[...]
    moments = []
    for turn in range(3):
        field = basis[turn]
        send_halo(turn, field)
        send_far(2 * turn)
        send_far(2 * turn + 1)
        if turn == 0:
            near.start()
        image = (4.0 + diag[...]) * field - neighbours(field)
        if turn == 0:
            moments.append(moment(field, field))
        for copy in halos[4 * turn :]:
            copy.wait_recv()
        image = image - ghosts([ring_in[4 * turn + side] for side in range(4)])
        basis[turn + 1] = image
        moments.append(moment(field, image))
        if turn < 2:
            moments.append(moment(image, image))
    part[...] = jnp.concatenate(moments + [jnp.zeros((2, S), F32)], axis=0)

    sums = []

    def exchange(source, slots, own, group, base):
        for i in range(7):
            copy = remote(
                source, slots.at[own], sum_send.at[base + i], sum_recv.at[base + i], group[i]
            )
            copy.start()
            sums.append(copy)
        slots[own] = source[...]

    exchange(part, plane_slots, q, plane_peer, 0)
    send_far(6)
    send_far(7)

    loads[2].wait()
    loads[3].wait()
    pick = (iota((NL * 8, 4 * NL), 1) == lev * NL + iota((NL * 8, 4 * NL), 0) // 8).astype(BF16)
    spread = (iota((4 * NL, 32 * NL), 0) == iota((4 * NL, 32 * NL), 1) // 8).astype(BF16)
    on = lax.rem(iota((NL * 8, 32 * NL), 0), 8) == lax.rem(iota((NL * 8, 32 * NL), 1), 8)
    high = inverse[...].astype(BF16)
    low = (inverse[...] - high.astype(F32)).astype(BF16)
    picked = []
    for index, piece in enumerate((high, low)):
        rows = dot_t(pick, piece)
        picked.append(rows)
        wide = dot(rows.astype(BF16), spread)
        kron[pl.ds(index * NL * 8, NL * 8), :] = jnp.where(on, wide, 0.0).astype(BF16)
    exact = dot_t(pick.astype(F32), inverse[...], HIGHEST)
    weight[...] = jnp.broadcast_to(
        jnp.sum(exact * thick[...], axis=1, keepdims=True), (NL * 8, S)
    )

    for copy in sums[:7]:
        copy.wait_recv()
    total = plane_slots[0]
    for i in range(1, 8):
        total = total + plane_slots[i]
    plane_total[...] = total
    exchange(plane_total, z_slots, z, z_peer, 7)
    for chunk in range(8, NC):
        send_far(chunk)
    for copy in sums[7:]:
        copy.wait_recv()
    total = z_slots[0]
    for i in range(1, 8):
        total = total + z_slots[i]
    mu = jnp.broadcast_to(jnp.sum(total, axis=1, keepdims=True), (8, S))
    steps = step_lengths([mu[k : k + 1, :] for k in range(6)])
    rhs[...] = (steps[0] * basis[0] + steps[1] * basis[1]) + steps[2] * basis[2]
    save = pltpu.make_async_copy(rhs, answer.at[0], store_sem.at[0])
    save.start()

    hands = []
    loads[4].wait()
    near.wait()
    theirs = pl.ds(opposite * NL, NL)

    def multiply(chunk):
        rows = pl.ds(chunk * R, R)
        block = gathered[:, rows, :].reshape(4 * NL * R, S)
        upper = block.astype(BF16)
        lower = (block - upper.astype(F32)).astype(BF16)
        both = dot(kron[...], upper)
        value = both[: NL * 8] + (both[NL * 8 :] + dot(kron[pl.ds(0, NL * 8), :], lower))
        column = value.reshape(NL, R, S) + weight[...].reshape(NL, R, S) * rhs[rows, :][None]
        adjoint[:, rows, :] = column

    for chunk in range(NC):
        far[chunk].wait_recv()
        rows = pl.ds(chunk * R, R)
        copy = remote(
            gathered.at[theirs, rows, :],
            gathered.at[theirs, rows, :],
            hand_send.at[chunk],
            hand_recv.at[chunk],
            (t, partner),
        )
        copy.start()
        hands.append(copy)
        if chunk:
            hands[chunk - 1].wait_recv()
            multiply(chunk - 1)
    hands[NC - 1].wait_recv()
    multiply(NC - 1)

    loads[5].wait()

    strips_out[...] = jnp.zeros_like(strips_out)

    def strip(level, carry):
        value = adjoint[level]
        lines = (
            to_row(coef[1, level][:, 0:1].astype(F32) * value[:, 0:1]),
            to_row(coef[0, level][:, S - 1 : S].astype(F32) * value[:, S - 1 : S]),
            coef[3, level][0:1, :].astype(F32) * value[0:1, :],
            coef[2, level][S - 1 : S, :].astype(F32) * value[S - 1 : S, :],
        )
        for side in range(4):
            strips_out[side, pl.ds(level, 1), :] = lines[side]
        return carry

    lax.fori_loop(0, NL, strip, 0)
    ghost_copies = []
    for side in range(4):
        copy = remote(
            strips_out.at[side], strips_in.at[side],
            ghost_send.at[side], ghost_recv.at[side], halo[side],
        )
        copy.start()
        ghost_copies.append(copy)

    ocean = (1 - land[t]).astype(F32)

    def inner(level, carry):
        value = adjoint[level]
        east_c = coef[0, level].astype(F32)
        west_c = coef[1, level].astype(F32)
        north_c = coef[2, level].astype(F32)
        south_c = coef[3, level].astype(F32)
        out = value - (east_c + west_c + north_c + south_c) * value
        out = out + jnp.where(lane == S - 1, 0.0, pltpu.roll(west_c * value, S - 1, 1))
        out = out + jnp.where(lane == 0, 0.0, pltpu.roll(east_c * value, 1, 1))
        out = out + jnp.where(row == S - 1, 0.0, pltpu.roll(south_c * value, S - 1, 0))
        out = out + jnp.where(row == 0, 0.0, pltpu.roll(north_c * value, 1, 0))
        result[level] = ocean * out
        return carry

    lax.fori_loop(0, NL, inner, 0)
    for copy in ghost_copies:
        copy.wait_recv()
    for side in (2, 3):
        strips_in[side] = dot(strips_in[side], perm[side], HIGHEST)

    def outer(level, carry):
        at = pl.ds(level, 1)
        east = to_column(strips_in[0, at, :], 0)
        west = to_column(strips_in[1, at, :], 1)
        rim = (jnp.where(lane == S - 1, east, 0.0) + jnp.where(lane == 0, west, 0.0)) + (
            jnp.where(row == S - 1, strips_in[2, at, :], 0.0)
            + jnp.where(row == 0, strips_in[3, at, :], 0.0)
        )
        result[level] = result[level] + ocean * rim
        return carry

    lax.fori_loop(0, NL, outer, 0)
    done = pltpu.make_async_copy(result, theta.at[0], store_sem.at[1])
    done.start()
    for copy in halos + far + sums + hands + ghost_copies:
        copy.wait_send()
    save.wait()
    done.wait()


def local(cot, surface, helm, coef, inverse, thick, flips, land):
    vmem = pltpu.VMEM
    dma = pltpu.SemaphoreType.DMA
    anywhere = pl.BlockSpec(memory_space=pl.ANY)
    smem = pl.BlockSpec(memory_space=pltpu.SMEM)
    return pl.pallas_call(
        kernel,
        out_shape=(
            jax.ShapeDtypeStruct((1, NL, S, S), F32),
            jax.ShapeDtypeStruct((1, S, S), F32),
        ),
        in_specs=[smem, smem] + [anywhere] * 6,
        out_specs=(anywhere, anywhere),
        scratch_shapes=[
            vmem((4 * NL, S, S), F32),
            vmem((4, NL, S, S), BF16),
            vmem((S, S), F32),
            vmem((S, S), F32),
            vmem((4 * NL, 4 * NL), F32),
            vmem((1, 4 * NL), F32),
            vmem((4, S, S), F32),
            vmem((4, S, S), F32),
            vmem((12, 1, S), F32),
            vmem((12, 1, S), F32),
            vmem((8, S), F32),
            vmem((8, 8, S), F32),
            vmem((8, S), F32),
            vmem((8, 8, S), F32),
            vmem((2 * NL * 8, 4 * NL * 8), BF16),
            vmem((NL * 8, S), F32),
            vmem((NL, S, S), F32),
            vmem((4, 24, S), F32),
            vmem((4, 24, S), F32),
            vmem((NL, S, S), F32),
            dma((6,)),
            dma((NC,)),
            dma((NC,)),
            dma((1,)),
            dma((1,)),
            dma((NC,)),
            dma((NC,)),
            dma((12,)),
            dma((12,)),
            dma((14,)),
            dma((14,)),
            dma((4,)),
            dma((4,)),
            dma((2,)),
        ],
        compiler_params=pltpu.CompilerParams(collective_id=0, has_side_effects=True),
        name="adjoint_step",
    )(flips, land, cot, surface, helm, coef, inverse, thick.reshape(1, 4 * NL))


def solution(mesh):
    return jax.shard_map(
        local,
        mesh=mesh,
        in_specs=(
            P("tile", "lev", None, None),
            P("tile", None, None),
            P("tile", None, None),
            P("tile", None, "lev", None, None),
            P("tile", None, None),
            P(),
            P(),
            P(),
        ),
        out_specs=(P("tile", "lev", None, None), P("tile", None, None)),
        check_vma=False,
    )
```

```python
import functools

import jax
import jax.numpy as jnp
from jax import lax
from jax.experimental import pallas as pl
from jax.experimental.pallas import tpu as pltpu
from jax.sharding import PartitionSpec as P

MESH = pl.DeviceIdType.MESH
S = 128
NL = 22
R = 16
NC = S // R
ORDER = (0, NC - 1) + tuple(range(1, NC - 1))
F32 = jnp.float32
BF16 = jnp.bfloat16
HIGHEST = lax.Precision.HIGHEST


def dot(a, b, precision=None):
    return lax.dot_general(
        a, b, (((1,), (0,)), ((), ())), precision=precision, preferred_element_type=F32
    )


def dot_t(a, b, precision=None):
    return lax.dot_general(
        a, b, (((1,), (1,)), ((), ())), precision=precision, preferred_element_type=F32
    )


def iota(shape, axis):
    return lax.broadcasted_iota(jnp.int32, shape, axis)


def step_lengths(mu):
    def product(a, b, power):
        total = None
        for i, x in enumerate(a):
            for j, y in enumerate(b):
                if x is not None and y is not None:
                    term = x * y * mu[i + j + power]
                    total = term if total is None else total + term
        return total

    one = jnp.ones_like(mu[0])
    residual, direction = [one, None, None], [one, None, None]
    answer = [None, None, None]
    norm = mu[0]
    for step in range(3):
        curvature = product(direction, direction, 1)
        alpha = norm / curvature
        if step:
            alpha = jnp.where(
                jnp.logical_and(norm > 0, curvature > 0), jnp.clip(alpha, 0.1, 21.0), 0.0
            )
        for i in range(step + 1):
            term = alpha * direction[i]
            answer[i] = term if answer[i] is None else answer[i] + term
        if step < 2:
            for i in range(step, -1, -1):
                term = alpha * direction[i]
                residual[i + 1] = -term if residual[i + 1] is None else residual[i + 1] - term
            new = product(residual, residual, 0)
            beta = jnp.where(norm > 0, jnp.maximum(new, 0.0) / norm, 0.0)
            direction = [
                None if r is None else (r if d is None else r + beta * d)
                for r, d in zip(residual, direction)
            ]
            norm = new
    return answer


def kernel(
    flips,
    land,
    cot,
    surface,
    helm,
    coef_hbm,
    inverse_hbm,
    thick_hbm,
    theta,
    answer,
    gathered,
    coef,
    diag,
    inverse,
    thick,
    basis,
    perm,
    ring_out,
    ring_in,
    part,
    plane_slots,
    plane_total,
    z_slots,
    kron,
    weight,
    edges,
    edge_coef,
    edge_matrix,
    edge_weight,
    adjoint,
    northward,
    southward,
    rim,
    strips_out,
    strips_in,
    load_sem,
    far_send,
    far_recv,
    near_send,
    near_recv,
    edge_send,
    edge_recv,
    hand_send,
    hand_recv,
    halo_send,
    halo_recv,
    sum_send,
    sum_recv,
    ghost_send,
    ghost_recv,
):
    t = lax.axis_index("tile")
    lev = lax.axis_index("lev")
    opposite = lax.rem(lev + 2, 4)
    partner = lev + 1 - 2 * lax.rem(lev, 2)
    z = t // 8
    q = lax.rem(t, 8)
    halo = [
        (lax.rem(t + 63, 64), lev),
        (lax.rem(t + 1, 64), lev),
        (lax.rem(t + 60, 64), lev),
        (lax.rem(t + 4, 64), lev),
    ]
    plane_peer = [(z * 8 + lax.rem(q + i, 8), lev) for i in range(1, 8)]
    z_peer = [(lax.rem(t + 8 * i, 64), lev) for i in range(1, 8)]

    barrier = pltpu.get_barrier_semaphore()
    peers = halo + plane_peer + z_peer + [(t, opposite), (t, partner)]
    for peer in peers:
        pl.semaphore_signal(barrier, inc=1, device_id=peer, device_id_type=MESH)

    def remote(src, dst, send, recv, peer):
        return pltpu.make_async_remote_copy(
            src_ref=src, dst_ref=dst, send_sem=send, recv_sem=recv,
            device_id=peer, device_id_type=MESH,
        )

    mine = pl.ds(lev * NL, NL)
    loads = [
        pltpu.make_async_copy(surface.at[0], basis.at[0], load_sem.at[0]),
        pltpu.make_async_copy(helm.at[0], diag, load_sem.at[1]),
        pltpu.make_async_copy(inverse_hbm.at[0], inverse, load_sem.at[2]),
        pltpu.make_async_copy(thick_hbm, thick, load_sem.at[3]),
        pltpu.make_async_copy(cot.at[0], gathered.at[mine], load_sem.at[4]),
        pltpu.make_async_copy(coef_hbm.at[0], coef, load_sem.at[5]),
    ]
    for load in loads:
        load.start()

    row = iota((S, S), 0)
    lane = iota((S, S), 1)
    eye = (row == lane).astype(F32)
    anti = (row + lane == S - 1).astype(F32)
    for side in range(4):
        perm[side] = jnp.where(flips[side, t] == 1, anti, eye)

    far = {}

    def send_far(chunk):
        rows = pl.ds(chunk * R, R)
        copy = remote(
            cot.at[0, :, rows, :],
            gathered.at[mine, rows, :],
            far_send.at[chunk],
            far_recv.at[chunk],
            (t, opposite),
        )
        copy.start()
        far[chunk] = copy

    def to_row(column):
        return jnp.sum(jnp.broadcast_to(column, (S, S)) * eye, axis=0, keepdims=True)

    halos = []

    def send_halo(turn, field):
        strips = (
            to_row(field[:, 0:1]),
            to_row(field[:, S - 1 : S]),
            field[0:1, :],
            field[S - 1 : S, :],
        )
        for side in range(4):
            slot = turn * 4 + side
            ring_out[slot] = strips[side]
        for side in range(4):
            slot = turn * 4 + side
            copy = remote(
                ring_out.at[slot], ring_in.at[slot],
                halo_send.at[slot], halo_recv.at[slot], halo[side],
            )
            copy.start()
            halos.append(copy)

    def neighbours(field):
        east = jnp.where(lane == S - 1, 0.0, pltpu.roll(field, S - 1, 1))
        west = jnp.where(lane == 0, 0.0, pltpu.roll(field, 1, 1))
        north = jnp.where(row == S - 1, 0.0, pltpu.roll(field, S - 1, 0))
        south = jnp.where(row == 0, 0.0, pltpu.roll(field, 1, 0))
        return (east + west) + (north + south)

    def to_column(line, side):
        return jnp.sum(perm[side] * line, axis=1, keepdims=True)

    def turned(line, side):
        return dot(jnp.broadcast_to(line, (8, S)), perm[side], HIGHEST)[0:1, :]

    def ghosts(lines):
        return (
            jnp.where(lane == S - 1, to_column(lines[0], 0), 0.0)
            + jnp.where(lane == 0, to_column(lines[1], 1), 0.0)
        ) + (
            jnp.where(row == S - 1, turned(lines[2], 2), 0.0)
            + jnp.where(row == 0, turned(lines[3], 3), 0.0)
        )

    def moment(a, b):
        return jnp.sum(a * b, axis=0, keepdims=True)

    loads[0].wait()
    loads[1].wait()
    pl.semaphore_wait(barrier, len(peers))

    near = remote(
        cot.at[0], gathered.at[mine], near_send.at[0], near_recv.at[0], (t, partner)
    )
    mine_edges = edges.at[lev]
    their_edges = edges.at[opposite]
    edge_copies = [
        remote(mine_edges, mine_edges, edge_send.at[0], edge_recv.at[0], (t, opposite)),
        remote(mine_edges, mine_edges, edge_send.at[1], edge_recv.at[1], (t, partner)),
        remote(their_edges, their_edges, edge_send.at[2], edge_recv.at[2], (t, partner)),
    ]

    def cotangent_edges():
        loads[4].wait()
        edges[lev] = jnp.zeros((2, 24, S), F32)

        def body(level, carry):
            at = pl.ds(level, 1)
            plane = gathered[lev * NL + level]
            edges[lev, 0, at, :] = to_row(plane[:, 0:1])
            edges[lev, 1, at, :] = to_row(plane[:, S - 1 : S])
            return carry

        lax.fori_loop(0, NL, body, 0, unroll=2)
        edge_copies[0].start()
        edge_copies[1].start()

    def coefficient_edges():
        loads[5].wait()
        edge_coef[...] = jnp.zeros((2, 24, S), F32)

        def body(level, carry):
            at = pl.ds(level, 1)
            edge_coef[0, at, :] = to_row(coef[1, level][:, 0:1].astype(F32))
            edge_coef[1, at, :] = to_row(coef[0, level][:, S - 1 : S].astype(F32))
            return carry

        lax.fori_loop(0, NL, body, 0, unroll=2)

    def build_kron():
        loads[2].wait()
        shape = (NL * 8, 32 * NL)
        pick = iota((NL * 8, 4 * NL), 1) == lev * NL + iota((NL * 8, 4 * NL), 0) // 8
        pick = pick.astype(BF16)
        spread = (iota((4 * NL, 32 * NL), 0) == iota((4 * NL, 32 * NL), 1) // 8).astype(BF16)
        on = lax.rem(iota(shape, 0), 8) == lax.rem(iota(shape, 1), 8)
        high = inverse[...].astype(BF16)
        low = (inverse[...] - high.astype(F32)).astype(BF16)
        for index, piece in enumerate((high, low)):
            wide = dot(dot_t(pick, piece).astype(BF16), spread)
            kron[pl.ds(index * NL * 8, NL * 8), :] = jnp.where(on, wide, 0.0).astype(BF16)

    def build_weights():
        loads[3].wait()
        pick = iota((NL * R, 4 * NL), 1) == lev * NL + iota((NL * R, 4 * NL), 0) // R
        exact = dot_t(pick.astype(F32), inverse[...], HIGHEST)
        total = jnp.sum(exact * thick[...], axis=1, keepdims=True)
        weight[...] = jnp.broadcast_to(total, (NL * R, S)).reshape(NL, R, S)
        shape = (24, 4 * NL)
        pick = jnp.logical_and(iota(shape, 1) == lev * NL + iota(shape, 0), iota(shape, 0) < NL)
        exact = dot_t(pick.astype(F32), inverse[...], HIGHEST)
        total = jnp.sum(exact * thick[...], axis=1, keepdims=True)
        edge_weight[...] = jnp.broadcast_to(total, (24, S))
        shape = (4 * NL, 96)
        place = iota(shape, 1)
        level = (place // 24) * NL + lax.rem(place, 24)
        widen = jnp.logical_and(level == iota(shape, 0), lax.rem(place, 24) < NL)
        edge_matrix[...] = dot(exact, widen.astype(F32), HIGHEST)

    moments = []
    for turn in range(3):
        field = basis[turn]
        send_halo(turn, field)
        if turn == 0:
            near.start()
            cotangent_edges()
        send_far(ORDER[turn])
        image = (4.0 + diag[...]) * field - neighbours(field)
        if turn == 0:
            moments.append(moment(field, field))
        elif turn == 1:
            build_kron()
        else:
            coefficient_edges()
        for copy in halos[4 * turn :]:
            copy.wait_recv()
        image = image - ghosts([ring_in[4 * turn + side] for side in range(4)])
        basis[turn + 1] = image
        moments.append(moment(field, image))
        if turn < 2:
            moments.append(moment(image, image))
    part[...] = jnp.concatenate(moments + [jnp.zeros((2, S), F32)], axis=0)

    sums = []

    def exchange(source, slots, own, group, base):
        for i in range(7):
            copy = remote(
                source, slots.at[own], sum_send.at[base + i], sum_recv.at[base + i], group[i]
            )
            copy.start()
            sums.append(copy)
        slots[own] = source[...]

    theirs = pl.ds(opposite * NL, NL)
    hands = {}

    def hand(chunk):
        far[chunk].wait_recv()
        rows = pl.ds(chunk * R, R)
        block = gathered.at[theirs, rows, :]
        copy = remote(block, block, hand_send.at[chunk], hand_recv.at[chunk], (t, partner))
        copy.start()
        hands[chunk] = copy

    def multiply(chunk):
        hands[chunk].wait_recv()
        halves = [gathered[:, pl.ds(chunk * R + i, 8), :].reshape(32 * NL, S) for i in (0, 8)]
        block = jnp.concatenate(halves, axis=1)
        upper = block.astype(BF16)
        lower = (block - upper.astype(F32)).astype(BF16)
        both = dot(kron[...], upper)
        value = both[: NL * 8] + (both[NL * 8 :] + dot(kron[pl.ds(0, NL * 8), :], lower))
        for i in (0, 1):
            half = value[:, i * S : (i + 1) * S].reshape(NL, 8, S)
            adjoint[:, pl.ds(chunk * R + 8 * i, 8), :] = half

    exchange(part, plane_slots, q, plane_peer, 0)
    send_far(ORDER[3])
    edge_copies[0].wait_recv()
    edge_copies[2].start()
    hand(ORDER[0])
    build_weights()
    for copy in sums[:7]:
        copy.wait_recv()
    total = plane_slots[0]
    for i in range(1, 8):
        total = total + plane_slots[i]
    plane_total[...] = total
    exchange(plane_total, z_slots, z, z_peer, 7)
    send_far(ORDER[4])
    near.wait()
    hand(ORDER[1])
    multiply(ORDER[0])
    multiply(ORDER[1])
    for copy in sums[7:]:
        copy.wait_recv()
    total = z_slots[0]
    for i in range(1, 8):
        total = total + z_slots[i]
    mu = jnp.broadcast_to(jnp.sum(total, axis=1, keepdims=True), (8, S))
    steps = step_lengths([mu[k : k + 1, :] for k in range(6)])
    field = (steps[0] * basis[0] + steps[1] * basis[1]) + steps[2] * basis[2]
    answer[0] = field

    ghost_copies = [
        remote(
            strips_out.at[side], strips_in.at[side],
            ghost_send.at[side], ghost_recv.at[side], halo[side],
        )
        for side in range(4)
    ]
    edge_copies[1].wait_recv()
    edge_copies[2].wait_recv()
    for side, column in enumerate((field[:, 0:1], field[:, S - 1 : S])):
        value = dot(edge_matrix[...], edges[:, side].reshape(96, S), HIGHEST)
        value = value + edge_weight[...] * to_row(column)
        strips_out[side] = value * edge_coef[side]
    ghost_copies[0].start()
    ghost_copies[1].start()
    send_far(ORDER[5])

    ocean = (1 - land[t]).astype(F32)
    wide = (NL, R, S)
    wide_lane = iota(wide, 2)

    def products(chunk):
        rows = pl.ds(chunk * R, R)
        value = adjoint[:, rows, :] + weight[...] * answer[0, rows, :][None]
        east_c = coef[0, :, rows, :].astype(F32)
        west_c = coef[1, :, rows, :].astype(F32)
        north_c = coef[2, :, rows, :].astype(F32)
        south_c = coef[3, :, rows, :].astype(F32)
        northward[:, pl.ds(8 + chunk * R, R), :] = north_c * value
        southward[:, rows, :] = south_c * value
        out = value - ((east_c + west_c) + (north_c + south_c)) * value
        out = out + jnp.where(wide_lane == S - 1, 0.0, pltpu.roll(west_c * value, S - 1, 2))
        out = out + jnp.where(wide_lane == 0, 0.0, pltpu.roll(east_c * value, 1, 2))
        theta[0, :, rows, :] = out

    def finish(chunk):
        rows = pl.ds(chunk * R, R)
        after = southward[:, pl.ds(chunk * R + 1, R), :]
        before = northward[:, pl.ds(chunk * R + 7, R), :]
        theta[0, :, rows, :] = ocean * (
            (theta[0, :, rows, :] + rim[:, rows, :]) + (after + before)
        )

    products(ORDER[0])
    products(ORDER[1])
    strips_out[2] = jnp.zeros((24, S), F32)
    strips_out[3] = jnp.zeros((24, S), F32)
    strips_out[2, pl.ds(0, NL), :] = southward[:, 0, :]
    strips_out[3, pl.ds(0, NL), :] = northward[:, 8 + S - 1, :]
    ghost_copies[2].start()
    ghost_copies[3].start()
    send_far(ORDER[6])
    send_far(ORDER[7])
    for chunk in ORDER[2:5]:
        hand(chunk)
    for chunk in ORDER[2:5]:
        multiply(chunk)
        products(chunk)

    for copy in ghost_copies:
        copy.wait_recv()

    def place(level, carry):
        at = pl.ds(level, 1)
        east = to_column(strips_in[0, at, :], 0)
        west = to_column(strips_in[1, at, :], 1)
        rim[level] = jnp.where(lane == S - 1, east, 0.0) + jnp.where(lane == 0, west, 0.0)
        return carry

    lax.fori_loop(0, NL, place, 0, unroll=2)
    southward[:, S, :] = dot(strips_in[2], perm[2], HIGHEST)[:NL]
    northward[:, 7, :] = dot(strips_in[3], perm[3], HIGHEST)[:NL]
    finish(0)
    finish(1)
    finish(2)
    hand(ORDER[5])
    multiply(ORDER[5])
    products(ORDER[5])
    finish(3)
    hand(ORDER[6])
    multiply(ORDER[6])
    products(ORDER[6])
    finish(4)
    hand(ORDER[7])
    multiply(ORDER[7])
    products(ORDER[7])
    for chunk in range(5, NC):
        finish(chunk)
    for copy in (
        halos + list(far.values()) + sums + list(hands.values()) + ghost_copies + edge_copies
    ):
        copy.wait_send()


def local(cot, surface, helm, coef, inverse, thick, flips, land):
    vmem = pltpu.VMEM
    dma = pltpu.SemaphoreType.DMA
    anywhere = pl.BlockSpec(memory_space=pl.ANY)
    smem = pl.BlockSpec(memory_space=pltpu.SMEM)
    return pl.pallas_call(
        kernel,
        out_shape=(
            pltpu.VMEM((1, NL, S, S), F32),
            pltpu.VMEM((1, S, S), F32),
        ),
        in_specs=[smem, smem] + [anywhere] * 6,
        out_specs=(pl.BlockSpec(memory_space=pltpu.VMEM),) * 2,
        scratch_shapes=[
            vmem((4 * NL, S, S), F32),
            vmem((4, NL, S, S), BF16),
            vmem((S, S), F32),
            vmem((4 * NL, 4 * NL), F32),
            vmem((1, 4 * NL), F32),
            vmem((4, S, S), F32),
            vmem((4, S, S), F32),
            vmem((12, 1, S), F32),
            vmem((12, 1, S), F32),
            vmem((8, S), F32),
            vmem((8, 8, S), F32),
            vmem((8, S), F32),
            vmem((8, 8, S), F32),
            vmem((2 * NL * 8, 4 * NL * 8), BF16),
            vmem((NL, R, S), F32),
            vmem((4, 2, 24, S), F32),
            vmem((2, 24, S), F32),
            vmem((24, 96), F32),
            vmem((24, S), F32),
            vmem((NL, S, S), F32),
            vmem((NL, S + 16, S), F32),
            vmem((NL, S + 16, S), F32),
            vmem((NL, S, S), F32),
            vmem((4, 24, S), F32),
            vmem((4, 24, S), F32),
            dma((6,)),
            dma((NC,)),
            dma((NC,)),
            dma((1,)),
            dma((1,)),
            dma((3,)),
            dma((3,)),
            dma((NC,)),
            dma((NC,)),
            dma((12,)),
            dma((12,)),
            dma((14,)),
            dma((14,)),
            dma((4,)),
            dma((4,)),
        ],
        compiler_params=pltpu.CompilerParams(collective_id=0, has_side_effects=True),
        name="adjoint_step",
    )(flips.T, land, cot, surface, helm, coef, inverse, thick.reshape(1, 4 * NL))


def solution(mesh):
    return jax.shard_map(
        local,
        mesh=mesh,
        in_specs=(
            P("tile", "lev", None, None),
            P("tile", None, None),
            P("tile", None, None),
            P("tile", None, "lev", None, None),
            P("tile", None, None),
            P(),
            P(),
            P(),
        ),
        out_specs=(P("tile", "lev", None, None), P("tile", None, None)),
        check_vma=False,
    )
```

```python
import functools

import jax
import jax.numpy as jnp
from jax import lax
from jax.experimental import pallas as pl
from jax.experimental.pallas import tpu as pltpu
from jax.sharding import PartitionSpec as P

MESH = pl.DeviceIdType.MESH
S = 128
NL = 22
R = 16
NC = S // R
H = 8
ORDER = (0, NC - 1) + tuple(range(1, NC - 1))
QUEUE = tuple(c * (R // H) + i for c in ORDER for i in range(R // H))
PLAN = (1, 1, 1, 1, 0)
HEAD = sum(PLAN)
F32 = jnp.float32
BF16 = jnp.bfloat16
HIGHEST = lax.Precision.HIGHEST


def dot(a, b, precision=None):
    return lax.dot_general(
        a, b, (((1,), (0,)), ((), ())), precision=precision, preferred_element_type=F32
    )


def dot_t(a, b, precision=None):
    return lax.dot_general(
        a, b, (((1,), (1,)), ((), ())), precision=precision, preferred_element_type=F32
    )


def iota(shape, axis):
    return lax.broadcasted_iota(jnp.int32, shape, axis)


def step_lengths(mu):
    def product(a, b, power):
        total = None
        for i, x in enumerate(a):
            for j, y in enumerate(b):
                if x is not None and y is not None:
                    term = x * y * mu[i + j + power]
                    total = term if total is None else total + term
        return total

    one = jnp.ones_like(mu[0])
    residual, direction = [one, None, None], [one, None, None]
    answer = [None, None, None]
    norm = mu[0]
    for step in range(3):
        curvature = product(direction, direction, 1)
        alpha = norm / curvature
        if step:
            alpha = jnp.where(
                jnp.logical_and(norm > 0, curvature > 0), jnp.clip(alpha, 0.1, 21.0), 0.0
            )
        for i in range(step + 1):
            term = alpha * direction[i]
            answer[i] = term if answer[i] is None else answer[i] + term
        if step < 2:
            for i in range(step, -1, -1):
                term = alpha * direction[i]
                residual[i + 1] = -term if residual[i + 1] is None else residual[i + 1] - term
            new = product(residual, residual, 0)
            beta = jnp.where(norm > 0, jnp.maximum(new, 0.0) / norm, 0.0)
            direction = [
                None if r is None else (r if d is None else r + beta * d)
                for r, d in zip(residual, direction)
            ]
            norm = new
    return answer


def kernel(
    flips,
    land,
    cot,
    surface,
    helm,
    coef_hbm,
    inverse_hbm,
    thick_hbm,
    theta,
    answer,
    gathered,
    coef,
    diag,
    solved,
    inverse,
    thick,
    basis,
    perm,
    ring_out,
    ring_in,
    part,
    plane_slots,
    plane_total,
    z_slots,
    kron,
    weight,
    edges,
    edge_coef,
    edge_matrix,
    edge_weight,
    adjoint,
    northward,
    southward,
    rim,
    strips_out,
    strips_in,
    load_sem,
    far_send,
    far_recv,
    near_send,
    near_recv,
    edge_send,
    edge_recv,
    hand_send,
    hand_recv,
    halo_send,
    halo_recv,
    sum_send,
    sum_recv,
    ghost_send,
    ghost_recv,
    solved_send,
    solved_recv,
):
    t = lax.axis_index("tile")
    lev = lax.axis_index("lev")
    solver = lax.rem(lev, 2) == 1
    opposite = lax.rem(lev + 2, 4)
    partner = lev + 1 - 2 * lax.rem(lev, 2)
    z = t // 8
    q = lax.rem(t, 8)
    halo = [
        (lax.rem(t + 63, 64), lev),
        (lax.rem(t + 1, 64), lev),
        (lax.rem(t + 60, 64), lev),
        (lax.rem(t + 4, 64), lev),
    ]
    plane_peer = [(z * 8 + lax.rem(q + i, 8), lev) for i in range(1, 8)]
    z_peer = [(lax.rem(t + 8 * i, 64), lev) for i in range(1, 8)]

    barrier = pltpu.get_barrier_semaphore()
    peers = halo + plane_peer + z_peer + [(t, opposite), (t, partner)]
    for peer in peers:
        pl.semaphore_signal(barrier, inc=1, device_id=peer, device_id_type=MESH)

    def remote(src, dst, send, recv, peer):
        return pltpu.make_async_remote_copy(
            src_ref=src, dst_ref=dst, send_sem=send, recv_sem=recv,
            device_id=peer, device_id_type=MESH,
        )

    mine = pl.ds(lev * NL, NL)
    loads = [
        pltpu.make_async_copy(surface.at[0], basis.at[0], load_sem.at[0]),
        pltpu.make_async_copy(helm.at[0], diag, load_sem.at[1]),
        pltpu.make_async_copy(inverse_hbm.at[0], inverse, load_sem.at[2]),
        pltpu.make_async_copy(thick_hbm, thick, load_sem.at[3]),
        pltpu.make_async_copy(cot.at[0], gathered.at[mine], load_sem.at[4]),
        pltpu.make_async_copy(coef_hbm.at[0], coef, load_sem.at[5]),
    ]
    for load in loads:
        load.start()

    row = iota((S, S), 0)
    lane = iota((S, S), 1)
    eye = (row == lane).astype(F32)
    anti = (row + lane == S - 1).astype(F32)
    for side in range(4):
        perm[side] = jnp.where(flips[side, t] == 1, anti, eye)

    def far(piece):
        rows = pl.ds(piece * H, H)
        return remote(
            cot.at[0, :, rows, :],
            gathered.at[mine, rows, :],
            far_send.at[piece],
            far_recv.at[piece],
            (t, opposite),
        )

    def send_far(pieces):
        for piece in pieces:
            far(piece).start()

    def to_row(column):
        return jnp.sum(jnp.broadcast_to(column, (S, S)) * eye, axis=0, keepdims=True)

    def fill_halo(turn, field):
        strips = (
            to_row(field[:, 0:1]),
            to_row(field[:, S - 1 : S]),
            field[0:1, :],
            field[S - 1 : S, :],
        )
        for side in range(4):
            slot = turn * 4 + side
            ring_out[slot] = strips[side]

    def halo_copy(turn, side):
        slot = turn * 4 + side
        return remote(
            ring_out.at[slot], ring_in.at[slot],
            halo_send.at[slot], halo_recv.at[slot], halo[side],
        )

    def send_halo(turn):
        for side in range(4):
            halo_copy(turn, side).start()

    def neighbours(field):
        east = jnp.where(lane == S - 1, 0.0, pltpu.roll(field, S - 1, 1))
        west = jnp.where(lane == 0, 0.0, pltpu.roll(field, 1, 1))
        north = jnp.where(row == S - 1, 0.0, pltpu.roll(field, S - 1, 0))
        south = jnp.where(row == 0, 0.0, pltpu.roll(field, 1, 0))
        return (east + west) + (north + south)

    def to_column(line, side):
        return jnp.sum(perm[side] * line, axis=1, keepdims=True)

    def turned(line, side):
        return dot(jnp.broadcast_to(line, (8, S)), perm[side], HIGHEST)[0:1, :]

    def ghosts(lines):
        return (
            jnp.where(lane == S - 1, to_column(lines[0], 0), 0.0)
            + jnp.where(lane == 0, to_column(lines[1], 1), 0.0)
        ) + (
            jnp.where(row == S - 1, turned(lines[2], 2), 0.0)
            + jnp.where(row == 0, turned(lines[3], 3), 0.0)
        )

    def moment(a, b):
        return jnp.sum(a * b, axis=0, keepdims=True)

    pl.semaphore_wait(barrier, len(peers))
    near = remote(
        cot.at[0], gathered.at[mine], near_send.at[0], near_recv.at[0], (t, partner)
    )
    mine_edges = edges.at[lev]
    their_edges = edges.at[opposite]
    edge_copies = [
        remote(mine_edges, mine_edges, edge_send.at[0], edge_recv.at[0], (t, opposite)),
        remote(mine_edges, mine_edges, edge_send.at[1], edge_recv.at[1], (t, partner)),
        remote(their_edges, their_edges, edge_send.at[2], edge_recv.at[2], (t, partner)),
    ]

    def cotangent_edges():
        loads[4].wait()
        edges[lev] = jnp.zeros((2, 24, S), F32)

        def body(level, carry):
            at = pl.ds(level, 1)
            plane = gathered[lev * NL + level]
            edges[lev, 0, at, :] = to_row(plane[:, 0:1])
            edges[lev, 1, at, :] = to_row(plane[:, S - 1 : S])
            return carry

        lax.fori_loop(0, NL, body, 0, unroll=2)
        edge_copies[0].start()
        edge_copies[1].start()

    def coefficient_edges():
        loads[5].wait()
        edge_coef[...] = jnp.zeros((2, 24, S), F32)

        def body(level, carry):
            at = pl.ds(level, 1)
            edge_coef[0, at, :] = to_row(coef[1, level][:, 0:1].astype(F32))
            edge_coef[1, at, :] = to_row(coef[0, level][:, S - 1 : S].astype(F32))
            return carry

        lax.fori_loop(0, NL, body, 0, unroll=2)

    def build_kron():
        loads[2].wait()
        shape = (NL * 8, 32 * NL)
        pick = iota((NL * 8, 4 * NL), 1) == lev * NL + iota((NL * 8, 4 * NL), 0) // 8
        pick = pick.astype(BF16)
        spread = (iota((4 * NL, 32 * NL), 0) == iota((4 * NL, 32 * NL), 1) // 8).astype(BF16)
        on = lax.rem(iota(shape, 0), 8) == lax.rem(iota(shape, 1), 8)
        high = inverse[...].astype(BF16)
        low = (inverse[...] - high.astype(F32)).astype(BF16)
        for index, piece in enumerate((high, low)):
            wide = dot(dot_t(pick, piece).astype(BF16), spread)
            kron[pl.ds(index * NL * 8, NL * 8), :] = jnp.where(on, wide, 0.0).astype(BF16)

    def build_weights():
        loads[3].wait()
        pick = iota((NL * R, 4 * NL), 1) == lev * NL + iota((NL * R, 4 * NL), 0) // R
        exact = dot_t(pick.astype(F32), inverse[...], HIGHEST)
        total = jnp.sum(exact * thick[...], axis=1, keepdims=True)
        weight[...] = jnp.broadcast_to(total, (NL * R, S)).reshape(NL, R, S)
        shape = (24, 4 * NL)
        pick = jnp.logical_and(iota(shape, 1) == lev * NL + iota(shape, 0), iota(shape, 0) < NL)
        exact = dot_t(pick.astype(F32), inverse[...], HIGHEST)
        total = jnp.sum(exact * thick[...], axis=1, keepdims=True)
        edge_weight[...] = jnp.broadcast_to(total, (24, S))
        shape = (4 * NL, 96)
        place = iota(shape, 1)
        level = (place // 24) * NL + lax.rem(place, 24)
        widen = jnp.logical_and(level == iota(shape, 0), lax.rem(place, 24) < NL)
        edge_matrix[...] = dot(exact, widen.astype(F32), HIGHEST)

    theirs = pl.ds(opposite * NL, NL)

    def hand_copy(piece):
        block = gathered.at[theirs, pl.ds(piece * H, H), :]
        return remote(block, block, hand_send.at[piece], hand_recv.at[piece], (t, partner))

    def hand_piece(piece):
        far(piece).wait_recv()
        hand_copy(piece).start()

    def split(rows):
        block = gathered[:, rows, :].reshape(32 * NL, S)
        upper = block.astype(BF16)
        return upper, (block - upper.astype(F32)).astype(BF16)

    def project(upper, lower):
        both = dot(kron[...], upper)
        return both[: NL * 8] + (both[NL * 8 :] + dot(kron[pl.ds(0, NL * 8), :], lower))

    def multiply(chunk):
        pieces = [chunk * 2, chunk * 2 + 1]
        for piece in pieces:
            hand_copy(piece).wait_recv()
        parts = [split(pl.ds(piece * H, H)) for piece in pieces]
        upper, lower = (jnp.concatenate(pair, axis=1) for pair in zip(*parts))
        value = project(upper, lower)
        for i, piece in enumerate(pieces):
            half = value[:, i * S : (i + 1) * S].reshape(NL, H, S)
            adjoint[:, pl.ds(piece * H, H), :] = half

    def multiply_piece(piece):
        hand_copy(piece).wait_recv()
        rows = pl.ds(piece * H, H)
        adjoint[:, rows, :] = project(*split(rows)).reshape(NL, H, S)

    def sum_copies(source, slots, own, group, base):
        return [
            remote(source, slots.at[own], sum_send.at[base + i], sum_recv.at[base + i], group[i])
            for i in range(7)
        ]

    def exchange(source, slots, own, group, base, meanwhile):
        copies = sum_copies(source, slots, own, group, base)
        for copy in copies:
            copy.start()
        slots[own] = source[...]
        meanwhile()
        for copy in copies:
            copy.wait_recv()
        total = slots[0]
        for i in range(1, 8):
            total = total + slots[i]
        return total

    def forward_edges():
        edge_copies[0].wait_recv()
        edge_copies[2].start()

    solved_copy = remote(
        solved, solved, solved_send.at[0], solved_recv.at[0], (t, partner)
    )
    plan = []
    for count in PLAN:
        done = sum(len(p) for p in plan)
        plan.append(QUEUE[done : done + count])

    @pl.when(jnp.logical_not(solver))
    def _():
        send_far(QUEUE[:4])
        near.start()
        cotangent_edges()
        send_far(QUEUE[4:])
        build_kron()
        build_weights()
        coefficient_edges()
        forward_edges()
        for piece in QUEUE:
            hand_piece(piece)
        near.wait()
        multiply(ORDER[0])
        multiply(ORDER[1])
        solved_copy.wait_recv()
        for piece in QUEUE:
            far(piece).wait_send()

    @pl.when(solver)
    def _():
        loads[0].wait()
        moments = []
        for turn in range(3):
            field = basis[turn]
            fill_halo(turn, field)
            send_halo(turn)
            send_far(plan[turn])
            if turn == 0:
                near.start()
                loads[1].wait()
            image = (4.0 + diag[...]) * field - neighbours(field)
            if turn == 0:
                moments.append(moment(field, field))
                cotangent_edges()
            elif turn == 1:
                build_kron()
            else:
                coefficient_edges()
            for side in range(4):
                halo_copy(turn, side).wait_recv()
            image = image - ghosts([ring_in[4 * turn + side] for side in range(4)])
            basis[turn + 1] = image
            moments.append(moment(field, image))
            if turn < 2:
                moments.append(moment(image, image))
        part[...] = jnp.concatenate(moments + [jnp.zeros((2, S), F32)], axis=0)

        def during_plane():
            send_far(plan[3])
            forward_edges()
            for piece in QUEUE[: HEAD // 2]:
                hand_piece(piece)
            build_weights()

        plane_total[...] = exchange(part, plane_slots, q, plane_peer, 0, during_plane)

        def during_z():
            send_far(plan[4])
            for piece in QUEUE[HEAD // 2 : HEAD]:
                hand_piece(piece)
            near.wait()
            multiply(ORDER[0])
            multiply(ORDER[1])

        total = exchange(plane_total, z_slots, z, z_peer, 7, during_z)
        mu = jnp.broadcast_to(jnp.sum(total, axis=1, keepdims=True), (8, S))
        steps = step_lengths([mu[k : k + 1, :] for k in range(6)])
        solved[...] = (steps[0] * basis[0] + steps[1] * basis[1]) + steps[2] * basis[2]
        solved_copy.start()

    field = solved[...]
    answer[0] = field

    ghost_copies = [
        remote(
            strips_out.at[side], strips_in.at[side],
            ghost_send.at[side], ghost_recv.at[side], halo[side],
        )
        for side in range(4)
    ]
    edge_copies[1].wait_recv()
    edge_copies[2].wait_recv()
    for side, column in enumerate((field[:, 0:1], field[:, S - 1 : S])):
        value = dot(edge_matrix[...], edges[:, side].reshape(96, S), HIGHEST)
        value = value + edge_weight[...] * to_row(column)
        strips_out[side] = value * edge_coef[side]
    ghost_copies[0].start()
    ghost_copies[1].start()

    @pl.when(solver)
    def _():
        send_far(QUEUE[HEAD:])

    def hand_late(pieces):
        @pl.when(solver)
        def _():
            for piece in pieces:
                hand_piece(piece)


    ocean = (1 - land[t]).astype(F32)
    wide = (NL, R, S)
    wide_lane = iota(wide, 2)

    def products(chunk):
        rows = pl.ds(chunk * R, R)
        value = adjoint[:, rows, :] + weight[...] * answer[0, rows, :][None]
        east_c = coef[0, :, rows, :].astype(F32)
        west_c = coef[1, :, rows, :].astype(F32)
        north_c = coef[2, :, rows, :].astype(F32)
        south_c = coef[3, :, rows, :].astype(F32)
        northward[:, pl.ds(8 + chunk * R, R), :] = north_c * value
        southward[:, rows, :] = south_c * value
        out = value - ((east_c + west_c) + (north_c + south_c)) * value
        out = out + jnp.where(wide_lane == S - 1, 0.0, pltpu.roll(west_c * value, S - 1, 2))
        out = out + jnp.where(wide_lane == 0, 0.0, pltpu.roll(east_c * value, 1, 2))
        theta[0, :, rows, :] = out

    def finish(chunk):
        rows = pl.ds(chunk * R, R)
        after = southward[:, pl.ds(chunk * R + 1, R), :]
        before = northward[:, pl.ds(chunk * R + 7, R), :]
        theta[0, :, rows, :] = ocean * (
            (theta[0, :, rows, :] + rim[:, rows, :]) + (after + before)
        )

    products(ORDER[0])
    products(ORDER[1])
    strips_out[2] = jnp.zeros((24, S), F32)
    strips_out[3] = jnp.zeros((24, S), F32)
    strips_out[2, pl.ds(0, NL), :] = southward[:, 0, :]
    strips_out[3, pl.ds(0, NL), :] = northward[:, 8 + S - 1, :]
    ghost_copies[2].start()
    ghost_copies[3].start()
    for chunk in ORDER[2:4]:
        hand_late((2 * chunk, 2 * chunk + 1))
        multiply(chunk)
        products(chunk)

    for copy in ghost_copies:
        copy.wait_recv()

    def place(level, carry):
        at = pl.ds(level, 1)
        east = to_column(strips_in[0, at, :], 0)
        west = to_column(strips_in[1, at, :], 1)
        rim[level] = jnp.where(lane == S - 1, east, 0.0) + jnp.where(lane == 0, west, 0.0)
        return carry

    lax.fori_loop(0, NL, place, 0, unroll=2)
    southward[:, S, :] = dot(strips_in[2], perm[2], HIGHEST)[:NL]
    northward[:, 7, :] = dot(strips_in[3], perm[3], HIGHEST)[:NL]
    finish(0)
    finish(1)
    for i in (4, 5, 6):
        chunk = ORDER[i]
        hand_late((2 * chunk, 2 * chunk + 1))
        multiply(chunk)
        products(chunk)
        finish(chunk - 1)
    for piece in QUEUE[-2:]:
        hand_late((piece,))
        multiply_piece(piece)
    products(ORDER[7])
    for chunk in range(NC - 3, NC):
        finish(chunk)

    @pl.when(solver)
    def _():
        for turn in range(3):
            for side in range(4):
                halo_copy(turn, side).wait_send()
        for copy in sum_copies(part, plane_slots, q, plane_peer, 0):
            copy.wait_send()
        for copy in sum_copies(plane_total, z_slots, z, z_peer, 7):
            copy.wait_send()
        for piece in QUEUE:
            far(piece).wait_send()
        solved_copy.wait_send()

    @pl.when(jnp.logical_not(solver))
    def _():
        loads[0].wait()
        loads[1].wait()

    for piece in QUEUE:
        hand_copy(piece).wait_send()
    for copy in ghost_copies + edge_copies:
        copy.wait_send()


def write(theta_in, answer_in, theta, answer, sem):
    copies = [
        pltpu.make_async_copy(answer_in, answer, sem.at[0]),
        pltpu.make_async_copy(theta_in, theta, sem.at[1]),
    ]
    for copy in copies:
        copy.start()
    for copy in copies:
        copy.wait()


def local(cot, surface, helm, coef, inverse, thick, flips, land):
    vmem = pltpu.VMEM
    dma = pltpu.SemaphoreType.DMA
    anywhere = pl.BlockSpec(memory_space=pl.ANY)
    smem = pl.BlockSpec(memory_space=pltpu.SMEM)
    held = pl.pallas_call(
        kernel,
        out_shape=(
            pltpu.VMEM((1, NL, S, S), F32),
            pltpu.VMEM((1, S, S), F32),
        ),
        in_specs=[smem, smem] + [anywhere] * 6,
        out_specs=(pl.BlockSpec(memory_space=pltpu.VMEM),) * 2,
        scratch_shapes=[
            vmem((4 * NL, S, S), F32),
            vmem((4, NL, S, S), BF16),
            vmem((S, S), F32),
            vmem((S, S), F32),
            vmem((4 * NL, 4 * NL), F32),
            vmem((1, 4 * NL), F32),
            vmem((4, S, S), F32),
            vmem((4, S, S), F32),
            vmem((12, 1, S), F32),
            vmem((12, 1, S), F32),
            vmem((8, S), F32),
            vmem((8, 8, S), F32),
            vmem((8, S), F32),
            vmem((8, 8, S), F32),
            vmem((2 * NL * 8, 4 * NL * 8), BF16),
            vmem((NL, R, S), F32),
            vmem((4, 2, 24, S), F32),
            vmem((2, 24, S), F32),
            vmem((24, 96), F32),
            vmem((24, S), F32),
            vmem((NL, S, S), F32),
            vmem((NL, S + 16, S), F32),
            vmem((NL, S + 16, S), F32),
            vmem((NL, S, S), F32),
            vmem((4, 24, S), F32),
            vmem((4, 24, S), F32),
            dma((6,)),
            dma((S // H,)),
            dma((S // H,)),
            dma((1,)),
            dma((1,)),
            dma((3,)),
            dma((3,)),
            dma((S // H,)),
            dma((S // H,)),
            dma((12,)),
            dma((12,)),
            dma((14,)),
            dma((14,)),
            dma((4,)),
            dma((4,)),
            dma((1,)),
            dma((1,)),
        ],
        compiler_params=pltpu.CompilerParams(collective_id=0, has_side_effects=True),
        name="adjoint_step",
    )(flips.T, land, cot, surface, helm, coef, inverse, thick.reshape(1, 4 * NL))
    return pl.pallas_call(
        write,
        out_shape=(
            jax.ShapeDtypeStruct((1, NL, S, S), F32),
            jax.ShapeDtypeStruct((1, S, S), F32),
        ),
        in_specs=[anywhere] * 2,
        out_specs=(anywhere, anywhere),
        scratch_shapes=[dma((2,))],
        compiler_params=pltpu.CompilerParams(vmem_limit_bytes=1 << 20),
        name="write_out",
    )(*held)


def solution(mesh):
    return jax.shard_map(
        local,
        mesh=mesh,
        in_specs=(
            P("tile", "lev", None, None),
            P("tile", None, None),
            P("tile", None, None),
            P("tile", None, "lev", None, None),
            P("tile", None, None),
            P(),
            P(),
            P(),
        ),
        out_specs=(P("tile", "lev", None, None), P("tile", None, None)),
        check_vma=False,
    )
```

```python
import functools

import jax
import jax.numpy as jnp
from jax import lax
from jax.experimental import pallas as pl
from jax.experimental.pallas import tpu as pltpu
from jax.sharding import PartitionSpec as P

MESH = pl.DeviceIdType.MESH
S = 128
NL = 22
R = 16
NC = S // R
H = 8
ORDER = (0, NC - 1) + tuple(range(1, NC - 1))
QUEUE = tuple(c * (R // H) + i for c in ORDER for i in range(R // H))
PLAN = (1, 1, 1, 1, 0)
HEAD = sum(PLAN)
F32 = jnp.float32
BF16 = jnp.bfloat16
HIGHEST = lax.Precision.HIGHEST


def dot(a, b, precision=None):
    return lax.dot_general(
        a, b, (((1,), (0,)), ((), ())), precision=precision, preferred_element_type=F32
    )


def dot_t(a, b, precision=None):
    return lax.dot_general(
        a, b, (((1,), (1,)), ((), ())), precision=precision, preferred_element_type=F32
    )


def iota(shape, axis):
    return lax.broadcasted_iota(jnp.int32, shape, axis)


def step_lengths(mu):
    def product(a, b, power):
        total = None
        for i, x in enumerate(a):
            for j, y in enumerate(b):
                if x is not None and y is not None:
                    term = x * y * mu[i + j + power]
                    total = term if total is None else total + term
        return total

    one = jnp.ones_like(mu[0])
    residual, direction = [one, None, None], [one, None, None]
    answer = [None, None, None]
    norm = mu[0]
    for step in range(3):
        curvature = product(direction, direction, 1)
        alpha = norm / curvature
        if step:
            alpha = jnp.where(
                jnp.logical_and(norm > 0, curvature > 0), jnp.clip(alpha, 0.1, 21.0), 0.0
            )
        for i in range(step + 1):
            term = alpha * direction[i]
            answer[i] = term if answer[i] is None else answer[i] + term
        if step < 2:
            for i in range(step, -1, -1):
                term = alpha * direction[i]
                residual[i + 1] = -term if residual[i + 1] is None else residual[i + 1] - term
            new = product(residual, residual, 0)
            beta = jnp.where(norm > 0, jnp.maximum(new, 0.0) / norm, 0.0)
            direction = [
                None if r is None else (r if d is None else r + beta * d)
                for r, d in zip(residual, direction)
            ]
            norm = new
    return answer


def kernel(
    flips,
    land,
    cot,
    surface,
    helm,
    coef_hbm,
    inverse_hbm,
    thick_hbm,
    theta,
    answer,
    gathered,
    coef,
    diag,
    solved,
    inverse,
    thick,
    basis,
    perm,
    ring_out,
    ring_in,
    part,
    plane_slots,
    plane_total,
    z_slots,
    kron,
    weight,
    edges,
    edge_coef,
    edge_matrix,
    edge_weight,
    adjoint,
    northward,
    southward,
    rim,
    strips_out,
    strips_in,
    load_sem,
    far_send,
    far_recv,
    near_send,
    near_recv,
    edge_send,
    edge_recv,
    hand_send,
    hand_recv,
    halo_send,
    halo_recv,
    sum_send,
    sum_recv,
    ghost_send,
    ghost_recv,
    solved_send,
    solved_recv,
):
    t = lax.axis_index("tile")
    lev = lax.axis_index("lev")
    solver = lax.rem(lev, 2) == 1
    opposite = lax.rem(lev + 2, 4)
    partner = lev + 1 - 2 * lax.rem(lev, 2)
    z = t // 8
    q = lax.rem(t, 8)
    halo = [
        (lax.rem(t + 63, 64), lev),
        (lax.rem(t + 1, 64), lev),
        (lax.rem(t + 60, 64), lev),
        (lax.rem(t + 4, 64), lev),
    ]
    plane_peer = [(z * 8 + lax.rem(q + i, 8), lev) for i in range(1, 8)]
    z_peer = [(lax.rem(t + 8 * i, 64), lev) for i in range(1, 8)]

    barrier = pltpu.get_barrier_semaphore()
    peers = [(t, opposite), (t, partner)] + halo
    for peer in peers:
        pl.semaphore_signal(barrier, inc=1, device_id=peer, device_id_type=MESH)

    @pl.when(solver)
    def _():
        for peer in plane_peer + z_peer:
            pl.semaphore_signal(barrier, inc=1, device_id=peer, device_id_type=MESH)


    def remote(src, dst, send, recv, peer):
        return pltpu.make_async_remote_copy(
            src_ref=src, dst_ref=dst, send_sem=send, recv_sem=recv,
            device_id=peer, device_id_type=MESH,
        )

    mine = pl.ds(lev * NL, NL)
    loads = [
        pltpu.make_async_copy(surface.at[0], basis.at[0], load_sem.at[0]),
        pltpu.make_async_copy(helm.at[0], diag, load_sem.at[1]),
        pltpu.make_async_copy(inverse_hbm.at[0], inverse, load_sem.at[2]),
        pltpu.make_async_copy(thick_hbm, thick, load_sem.at[3]),
        pltpu.make_async_copy(cot.at[0], gathered.at[mine], load_sem.at[4]),
        pltpu.make_async_copy(coef_hbm.at[0], coef, load_sem.at[5]),
    ]
    for load in loads:
        load.start()

    row = iota((S, S), 0)
    lane = iota((S, S), 1)
    eye = (row == lane).astype(F32)
    anti = (row + lane == S - 1).astype(F32)

    def orient():
        for side in range(4):
            perm[side] = jnp.where(flips[side, t] == 1, anti, eye)

    def far(piece, count=1):
        rows = pl.ds(piece * H, count * H)
        return remote(
            cot.at[0, :, rows, :],
            gathered.at[mine, rows, :],
            far_send.at[piece],
            far_recv.at[piece],
            (t, opposite),
        )

    def send_far(pieces):
        for piece in pieces:
            far(piece).start()

    def to_row(column):
        return jnp.sum(jnp.broadcast_to(column, (S, S)) * eye, axis=0, keepdims=True)

    def fill_halo(turn, field):
        strips = (
            to_row(field[:, 0:1]),
            to_row(field[:, S - 1 : S]),
            field[0:1, :],
            field[S - 1 : S, :],
        )
        for side in range(4):
            slot = turn * 4 + side
            ring_out[slot] = strips[side]

    def halo_copy(turn, side):
        slot = turn * 4 + side
        return remote(
            ring_out.at[slot], ring_in.at[slot],
            halo_send.at[slot], halo_recv.at[slot], halo[side],
        )

    def send_halo(turn):
        for side in range(4):
            halo_copy(turn, side).start()

    def neighbours(field):
        east = jnp.where(lane == S - 1, 0.0, pltpu.roll(field, S - 1, 1))
        west = jnp.where(lane == 0, 0.0, pltpu.roll(field, 1, 1))
        north = jnp.where(row == S - 1, 0.0, pltpu.roll(field, S - 1, 0))
        south = jnp.where(row == 0, 0.0, pltpu.roll(field, 1, 0))
        return (east + west) + (north + south)

    def to_column(line, side):
        return jnp.sum(perm[side] * line, axis=1, keepdims=True)

    def turned(line, side):
        return dot(jnp.broadcast_to(line, (8, S)), perm[side], HIGHEST)[0:1, :]

    def ghosts(lines):
        return (
            jnp.where(lane == S - 1, to_column(lines[0], 0), 0.0)
            + jnp.where(lane == 0, to_column(lines[1], 1), 0.0)
        ) + (
            jnp.where(row == S - 1, turned(lines[2], 2), 0.0)
            + jnp.where(row == 0, turned(lines[3], 3), 0.0)
        )

    def moment(a, b):
        return jnp.sum(a * b, axis=0, keepdims=True)

    pl.semaphore_wait(barrier, len(peers) + jnp.where(solver, 14, 0))
    near = remote(
        cot.at[0], gathered.at[mine], near_send.at[0], near_recv.at[0], (t, partner)
    )
    mine_edges = edges.at[lev]
    their_edges = edges.at[opposite]
    edge_copies = [
        remote(mine_edges, mine_edges, edge_send.at[0], edge_recv.at[0], (t, opposite)),
        remote(mine_edges, mine_edges, edge_send.at[1], edge_recv.at[1], (t, partner)),
        remote(their_edges, their_edges, edge_send.at[2], edge_recv.at[2], (t, partner)),
    ]

    def cotangent_edges():
        loads[4].wait()
        edges[lev] = jnp.zeros((2, 24, S), F32)

        def body(level, carry):
            at = pl.ds(level, 1)
            plane = gathered[lev * NL + level]
            edges[lev, 0, at, :] = to_row(plane[:, 0:1])
            edges[lev, 1, at, :] = to_row(plane[:, S - 1 : S])
            return carry

        lax.fori_loop(0, NL, body, 0, unroll=2)
        edge_copies[0].start()
        edge_copies[1].start()

    def coefficient_edges():
        loads[5].wait()
        edge_coef[...] = jnp.zeros((2, 24, S), F32)

        def body(level, carry):
            at = pl.ds(level, 1)
            edge_coef[0, at, :] = to_row(coef[1, level][:, 0:1].astype(F32))
            edge_coef[1, at, :] = to_row(coef[0, level][:, S - 1 : S].astype(F32))
            return carry

        lax.fori_loop(0, NL, body, 0, unroll=2)

    def build_kron():
        loads[2].wait()
        shape = (NL * 8, 32 * NL)
        pick = iota((NL * 8, 4 * NL), 1) == lev * NL + iota((NL * 8, 4 * NL), 0) // 8
        pick = pick.astype(BF16)
        spread = (iota((4 * NL, 32 * NL), 0) == iota((4 * NL, 32 * NL), 1) // 8).astype(BF16)
        on = lax.rem(iota(shape, 0), 8) == lax.rem(iota(shape, 1), 8)
        high = inverse[...].astype(BF16)
        low = (inverse[...] - high.astype(F32)).astype(BF16)
        for index, piece in enumerate((high, low)):
            wide = dot(dot_t(pick, piece).astype(BF16), spread)
            kron[pl.ds(index * NL * 8, NL * 8), :] = jnp.where(on, wide, 0.0).astype(BF16)

    def build_weights():
        loads[3].wait()
        pick = iota((NL * R, 4 * NL), 1) == lev * NL + iota((NL * R, 4 * NL), 0) // R
        exact = dot_t(pick.astype(F32), inverse[...], HIGHEST)
        total = jnp.sum(exact * thick[...], axis=1, keepdims=True)
        weight[...] = jnp.broadcast_to(total, (NL * R, S)).reshape(NL, R, S)
        shape = (24, 4 * NL)
        pick = jnp.logical_and(iota(shape, 1) == lev * NL + iota(shape, 0), iota(shape, 0) < NL)
        exact = dot_t(pick.astype(F32), inverse[...], HIGHEST)
        total = jnp.sum(exact * thick[...], axis=1, keepdims=True)
        edge_weight[...] = jnp.broadcast_to(total, (24, S))
        shape = (4 * NL, 96)
        place = iota(shape, 1)
        level = (place // 24) * NL + lax.rem(place, 24)
        widen = jnp.logical_and(level == iota(shape, 0), lax.rem(place, 24) < NL)
        edge_matrix[...] = dot(exact, widen.astype(F32), HIGHEST)

    theirs = pl.ds(opposite * NL, NL)

    def hand_copy(piece):
        block = gathered.at[theirs, pl.ds(piece * H, H), :]
        return remote(block, block, hand_send.at[piece], hand_recv.at[piece], (t, partner))

    def hand_piece(piece):
        far(piece).wait_recv()
        hand_copy(piece).start()

    def hand_pair(chunk):
        far(2 * chunk, 2).wait_recv()
        hand_copy(2 * chunk).start()
        hand_copy(2 * chunk + 1).start()

    def split(rows):
        block = gathered[:, rows, :].reshape(32 * NL, S)
        upper = block.astype(BF16)
        return upper, (block - upper.astype(F32)).astype(BF16)

    def project(upper, lower):
        both = dot(kron[...], upper)
        return both[: NL * 8] + (both[NL * 8 :] + dot(kron[pl.ds(0, NL * 8), :], lower))

    def multiply(chunk):
        pieces = [chunk * 2, chunk * 2 + 1]
        for piece in pieces:
            hand_copy(piece).wait_recv()
        parts = [split(pl.ds(piece * H, H)) for piece in pieces]
        upper, lower = (jnp.concatenate(pair, axis=1) for pair in zip(*parts))
        value = project(upper, lower)
        for i, piece in enumerate(pieces):
            half = value[:, i * S : (i + 1) * S].reshape(NL, H, S)
            adjoint[:, pl.ds(piece * H, H), :] = half

    def multiply_piece(piece):
        hand_copy(piece).wait_recv()
        rows = pl.ds(piece * H, H)
        adjoint[:, rows, :] = project(*split(rows)).reshape(NL, H, S)

    def sum_copies(source, slots, own, group, base):
        return [
            remote(source, slots.at[own], sum_send.at[base + i], sum_recv.at[base + i], group[i])
            for i in range(7)
        ]

    def exchange(source, slots, own, group, base, meanwhile):
        copies = sum_copies(source, slots, own, group, base)
        for copy in copies:
            copy.start()
        slots[own] = source[...]
        meanwhile()
        for copy in copies:
            copy.wait_recv()
        total = slots[0]
        for i in range(1, 8):
            total = total + slots[i]
        return total

    def forward_edges():
        edge_copies[0].wait_recv()
        edge_copies[2].start()

    solved_copy = remote(
        solved, solved, solved_send.at[0], solved_recv.at[0], (t, partner)
    )
    plan = []
    for count in PLAN:
        done = sum(len(p) for p in plan)
        plan.append(QUEUE[done : done + count])

    @pl.when(jnp.logical_not(solver))
    def _():
        for chunk in ORDER[:2]:
            far(2 * chunk, 2).start()
        near.start()
        orient()
        cotangent_edges()
        for chunk in ORDER[2:]:
            far(2 * chunk, 2).start()
        build_kron()
        build_weights()
        coefficient_edges()
        forward_edges()
        for chunk in ORDER:
            hand_pair(chunk)
        near.wait()
        multiply(ORDER[0])
        multiply(ORDER[1])
        solved_copy.wait_recv()
        for chunk in ORDER:
            far(2 * chunk, 2).wait_send()

    @pl.when(solver)
    def _():
        loads[0].wait()
        moments = []
        for turn in range(3):
            field = basis[turn]
            fill_halo(turn, field)
            send_halo(turn)
            send_far(plan[turn])
            if turn == 0:
                near.start()
                loads[1].wait()
                orient()
                moments.append(moment(field, field))
            else:
                moments.append(moment(basis[turn - 1], field))
                moments.append(moment(field, field))
            image = (4.0 + diag[...]) * field - neighbours(field)
            if turn == 0:
                cotangent_edges()
            elif turn == 1:
                build_kron()
            else:
                coefficient_edges()
            for side in range(4):
                halo_copy(turn, side).wait_recv()
            image = image - ghosts([ring_in[4 * turn + side] for side in range(4)])
            basis[turn + 1] = image
        moments.append(moment(basis[2], basis[3]))
        part[...] = jnp.concatenate(moments + [jnp.zeros((2, S), F32)], axis=0)

        def during_plane():
            send_far(plan[3])
            forward_edges()
            for piece in QUEUE[:2]:
                hand_piece(piece)
            build_weights()

        plane_total[...] = exchange(part, plane_slots, q, plane_peer, 0, during_plane)

        def during_z():
            send_far(plan[4])
            for piece in QUEUE[2:4]:
                hand_piece(piece)
            near.wait()
            multiply(ORDER[0])
            multiply(ORDER[1])

        total = exchange(plane_total, z_slots, z, z_peer, 7, during_z)
        mu = jnp.broadcast_to(jnp.sum(total, axis=1, keepdims=True), (8, S))
        steps = step_lengths([mu[k : k + 1, :] for k in range(6)])
        solved[...] = (steps[0] * basis[0] + steps[1] * basis[1]) + steps[2] * basis[2]
        solved_copy.start()

    field = solved[...]
    answer[0] = field

    ghost_copies = [
        remote(
            strips_out.at[side], strips_in.at[side],
            ghost_send.at[side], ghost_recv.at[side], halo[side],
        )
        for side in range(4)
    ]
    edge_copies[1].wait_recv()
    edge_copies[2].wait_recv()
    for side, column in enumerate((field[:, 0:1], field[:, S - 1 : S])):
        value = dot(edge_matrix[...], edges[:, side].reshape(96, S), HIGHEST)
        value = value + edge_weight[...] * to_row(column)
        strips_out[side] = value * edge_coef[side]
    ghost_copies[0].start()
    ghost_copies[1].start()

    @pl.when(solver)
    def _():
        for chunk in ORDER[2:7]:
            far(2 * chunk, 2).start()
        send_far(QUEUE[-2:])

    def hand_late(pieces):
        @pl.when(solver)
        def _():
            for piece in pieces:
                if len(pieces) == 1:
                    hand_piece(piece)
                elif piece % 2 == 0:
                    hand_pair(piece // 2)


    ocean = (1 - land[t]).astype(F32)
    wide = (NL, R, S)
    wide_lane = iota(wide, 2)

    def products(chunk):
        rows = pl.ds(chunk * R, R)
        value = adjoint[:, rows, :] + weight[...] * answer[0, rows, :][None]
        east_c = coef[0, :, rows, :].astype(F32)
        west_c = coef[1, :, rows, :].astype(F32)
        north_c = coef[2, :, rows, :].astype(F32)
        south_c = coef[3, :, rows, :].astype(F32)
        northward[:, pl.ds(8 + chunk * R, R), :] = north_c * value
        southward[:, rows, :] = south_c * value
        out = value - ((east_c + west_c) + (north_c + south_c)) * value
        out = out + jnp.where(wide_lane == S - 1, 0.0, pltpu.roll(west_c * value, S - 1, 2))
        out = out + jnp.where(wide_lane == 0, 0.0, pltpu.roll(east_c * value, 1, 2))
        theta[0, :, rows, :] = out

    def finish(chunk):
        rows = pl.ds(chunk * R, R)
        after = southward[:, pl.ds(chunk * R + 1, R), :]
        before = northward[:, pl.ds(chunk * R + 7, R), :]
        theta[0, :, rows, :] = ocean * (
            (theta[0, :, rows, :] + rim[:, rows, :]) + (after + before)
        )

    products(ORDER[0])
    products(ORDER[1])
    strips_out[2] = jnp.zeros((24, S), F32)
    strips_out[3] = jnp.zeros((24, S), F32)
    strips_out[2, pl.ds(0, NL), :] = southward[:, 0, :]
    strips_out[3, pl.ds(0, NL), :] = northward[:, 8 + S - 1, :]
    ghost_copies[2].start()
    ghost_copies[3].start()
    for chunk in ORDER[2:4]:
        hand_late((2 * chunk, 2 * chunk + 1))
        multiply(chunk)
        products(chunk)

    for copy in ghost_copies:
        copy.wait_recv()

    def place(level, carry):
        at = pl.ds(level, 1)
        east = to_column(strips_in[0, at, :], 0)
        west = to_column(strips_in[1, at, :], 1)
        rim[level] = jnp.where(lane == S - 1, east, 0.0) + jnp.where(lane == 0, west, 0.0)
        return carry

    lax.fori_loop(0, NL, place, 0, unroll=2)
    southward[:, S, :] = dot(strips_in[2], perm[2], HIGHEST)[:NL]
    northward[:, 7, :] = dot(strips_in[3], perm[3], HIGHEST)[:NL]
    finish(0)
    finish(1)
    for i in (4, 5, 6):
        chunk = ORDER[i]
        hand_late((2 * chunk, 2 * chunk + 1))
        multiply(chunk)
        products(chunk)
        finish(chunk - 1)
    for piece in QUEUE[-2:]:
        hand_late((piece,))
        multiply_piece(piece)
    products(ORDER[7])
    for chunk in range(NC - 3, NC):
        finish(chunk)

    @pl.when(solver)
    def _():
        for turn in range(3):
            for side in range(4):
                halo_copy(turn, side).wait_send()
        for copy in sum_copies(part, plane_slots, q, plane_peer, 0):
            copy.wait_send()
        for copy in sum_copies(plane_total, z_slots, z, z_peer, 7):
            copy.wait_send()
        for piece in QUEUE[:4] + QUEUE[-2:]:
            far(piece).wait_send()
        for chunk in ORDER[2:7]:
            far(2 * chunk, 2).wait_send()
        solved_copy.wait_send()

    @pl.when(jnp.logical_not(solver))
    def _():
        loads[0].wait()
        loads[1].wait()

    for piece in QUEUE:
        hand_copy(piece).wait_send()
    for copy in ghost_copies + edge_copies:
        copy.wait_send()


def write(theta_in, answer_in, theta, answer, sem):
    copies = [pltpu.make_async_copy(answer_in, answer, sem.at[4])]
    for i in range(4):
        part = pl.ds(6 * i, min(6, NL - 6 * i))
        copies.append(pltpu.make_async_copy(theta_in.at[0, part], theta.at[0, part], sem.at[i]))
    for copy in copies:
        copy.start()
    for copy in copies:
        copy.wait()


def local(cot, surface, helm, coef, inverse, thick, flips, land):
    vmem = pltpu.VMEM
    dma = pltpu.SemaphoreType.DMA
    anywhere = pl.BlockSpec(memory_space=pl.ANY)
    smem = pl.BlockSpec(memory_space=pltpu.SMEM)
    held = pl.pallas_call(
        kernel,
        out_shape=(
            pltpu.VMEM((1, NL, S, S), F32),
            pltpu.VMEM((1, S, S), F32),
        ),
        in_specs=[smem, smem] + [anywhere] * 6,
        out_specs=(pl.BlockSpec(memory_space=pltpu.VMEM),) * 2,
        scratch_shapes=[
            vmem((4 * NL, S, S), F32),
            vmem((4, NL, S, S), BF16),
            vmem((S, S), F32),
            vmem((S, S), F32),
            vmem((4 * NL, 4 * NL), F32),
            vmem((1, 4 * NL), F32),
            vmem((4, S, S), F32),
            vmem((4, S, S), F32),
            vmem((12, 1, S), F32),
            vmem((12, 1, S), F32),
            vmem((8, S), F32),
            vmem((8, 8, S), F32),
            vmem((8, S), F32),
            vmem((8, 8, S), F32),
            vmem((2 * NL * 8, 4 * NL * 8), BF16),
            vmem((NL, R, S), F32),
            vmem((4, 2, 24, S), F32),
            vmem((2, 24, S), F32),
            vmem((24, 96), F32),
            vmem((24, S), F32),
            vmem((NL, S, S), F32),
            vmem((NL, S + 16, S), F32),
            vmem((NL, S + 16, S), F32),
            vmem((NL, S, S), F32),
            vmem((4, 24, S), F32),
            vmem((4, 24, S), F32),
            dma((6,)),
            dma((S // H,)),
            dma((S // H,)),
            dma((1,)),
            dma((1,)),
            dma((3,)),
            dma((3,)),
            dma((S // H,)),
            dma((S // H,)),
            dma((12,)),
            dma((12,)),
            dma((14,)),
            dma((14,)),
            dma((4,)),
            dma((4,)),
            dma((1,)),
            dma((1,)),
        ],
        compiler_params=pltpu.CompilerParams(collective_id=0, has_side_effects=True),
        name="adjoint_step",
    )(flips.T, land, cot, surface, helm, coef, inverse, thick.reshape(1, 4 * NL))
    return pl.pallas_call(
        write,
        out_shape=(
            jax.ShapeDtypeStruct((1, NL, S, S), F32),
            jax.ShapeDtypeStruct((1, S, S), F32),
        ),
        in_specs=[anywhere] * 2,
        out_specs=(anywhere, anywhere),
        scratch_shapes=[dma((5,))],
        compiler_params=pltpu.CompilerParams(vmem_limit_bytes=1 << 20),
        name="write_out",
    )(*held)


def solution(mesh):
    return jax.shard_map(
        local,
        mesh=mesh,
        in_specs=(
            P("tile", "lev", None, None),
            P("tile", None, None),
            P("tile", None, None),
            P("tile", None, "lev", None, None),
            P("tile", None, None),
            P(),
            P(),
            P(),
        ),
        out_specs=(P("tile", "lev", None, None), P("tile", None, None)),
        check_vma=False,
    )
```
